32 devices in a mesh: section: 2 (over core), rep: 2 (over x), tp: 8 (over z, y).
Axes of the slice: x: 2, y: 2, z: 4, core: 2. Of those that a mesh axis runs over, the one named last changes fastest.
Arguments:
- states: bfloat16 [2, 2, 256, 8192], P('section', 'rep', None, 'tp'), may hold values from -6 to 6
- q_weight: bfloat16 [8192, 4096], P(None, 'tp'), may hold values from -0.0625 to 0.0625
- kv_weight: bfloat16 [8192, 1024], P('tp'), may hold values from -0.0625 to 0.0625
- o_weight: bfloat16 [4096, 8192], P(None, 'tp'), may hold values from -0.09375 to 0.09375
- store_keys: bfloat16 [2, 2, 4096, 512], P('section', 'rep', 'tp'), may hold values from -170 to 170
- store_values: bfloat16 [2, 2, 4096, 512], P('section', 'rep', 'tp'), may hold values from -48 to 48
- prefix_len: int32 [2], replicated, may hold values from 1024 to 4096
- cache_len: int32 [2, 4], P('rep'), may hold values from 128 to 1024
- parents: int32 [2, 4, 64], P('rep'), may hold values from -1 to 62, as said below
Outputs:
- attn_out: bfloat16 [2, 2, 256, 8192], P('section', 'rep', None, 'tp')
The draws below stay inside these ranges and needn't reach their ends.
Inputs may be any that keep to these rules, and one draw needn't show every extreme that they name: `parents`: each node's parent is an earlier node of the same tree; only node 0 has -1.
All inputs are finite; a program needn't handle non-finite values.
Results may differ from the reference program's by a relative error of at most 0.0065.
The reference program's roundings to bfloat16 on the way count: a program that leaves them out, or rounds other values in their place, can miss the bound.
Values may be sent and summed in bfloat16 or wider, within the bound.
No kernel may reach another device: no remote copies, remote signals or barrier semaphores. Data moves between devices by JAX's collectives and lax.ppermute only.
A program may use at most 128 MiB of HBM per device.

```python
import jax
import jax.numpy as jnp
from jax import lax

D = 8192
QH = 32
KVH = 4
HD = 128
SEQS = 4
NODES = 64
CACHE = 1024
ROWS = 256
CTX = 4096
QW = 4096
KW = 512
N_SECTION = 2
N_REP = 2
N_TP = 8


def draw_store_keys(key, part):
    full_shape = (N_SECTION, N_REP, CTX, KVH * HD)
    return jnp.clip(2.0 * jax.random.normal(key, full_shape, jnp.float32), -12.0, 12.0).astype(jnp.bfloat16)


def draw_parents(key, part):
    node_ids = jnp.arange(NODES, dtype=jnp.int32)
    offsets = jax.random.randint(key, (N_REP, SEQS, NODES), 1, 5, dtype=jnp.int32)
    return jnp.where(node_ids == 0, -1, jnp.maximum(node_ids - offsets, 0)).astype(jnp.int32)


def with_ends(entries, key, least, top_value):
    index_at = [jax.random.randint(jax.random.fold_in(key, axis), (), 0, length) for axis, length in enumerate(entries.shape)]
    longest = entries.shape.index(max(entries.shape))
    neighbour = index_at[:longest] + [(index_at[longest] + 1) % entries.shape[longest]] + index_at[longest + 1:]
    return entries.at[tuple(index_at)].set(least).at[tuple(neighbour)].set(top_value)


def levels(rng, dims, shards, low, largest):
    factor_of = 1.0
    for axis_at, blocks in shards:
        draws = jax.random.uniform(jax.random.fold_in(jax.random.fold_in(rng, 6), axis_at), (blocks,), jnp.float32, low / len(shards), largest / len(shards))
        factor_of = factor_of * jnp.repeat(jnp.exp(draws), dims[axis_at] // blocks).reshape((-1,) + (1,) * (len(dims) - 1 - axis_at))
    return factor_of


def gaussian(stream_key, extent, width, reach, shards=(), held_as=jnp.bfloat16):
    level = levels(stream_key, extent, shards, -0.22, 0.18) if shards else 1.0
    entries = jax.random.normal(stream_key, extent, jnp.float32) * width * level
    return jnp.minimum(jnp.maximum(entries, -reach), reach).astype(held_as)


def setup_inputs(seed: int = 0) -> dict:
    streams_of = jax.random.split(jax.random.key(seed), 10)
    return {
        "states": gaussian(streams_of[0], (N_SECTION, N_REP, ROWS, D), 1.0, 6.0, ((0, 2), (1, 2), (3, 8))),
        "q_weight": gaussian(streams_of[1], (D, QW), D ** -0.5, 0.0625, ((1, 8),)),
        "kv_weight": gaussian(streams_of[2], (D, 2 * KW), D ** -0.5, 0.0625, ((0, 8),)),
        "o_weight": gaussian(streams_of[3], (QW, D), QW ** -0.5, 0.09375, ((1, 8),)),
        "store_keys": draw_store_keys(jax.random.fold_in(streams_of[9], 71), 0),
        "store_values": gaussian(streams_of[5], (N_SECTION, N_REP, CTX, KW), 8.0, 48.0, ((0, 2), (1, 2), (2, 8))),
        "prefix_len": jax.random.randint(streams_of[6], (N_REP,), CTX // 4, CTX + 1).astype(jnp.int32),
        "cache_len": with_ends(jax.random.randint(streams_of[7], (N_REP, SEQS), CACHE // 8, CACHE + 1), jax.random.fold_in(streams_of[7], 1), CACHE // 8, CACHE).astype(jnp.int32),
        "parents": draw_parents(jax.random.fold_in(streams_of[9], 71), 0),
    }


ROPE_BASE = 500000.0
MASKED_SCORE = -1e30


def rotate(vectors, positions):
    head_size = vectors.shape[-1]
    half_width = head_size // 2
    exponent = jnp.arange(half_width, dtype=jnp.float32) * (-2.0 / head_size)
    frequency = jnp.exp(exponent * jnp.log(jnp.float32(ROPE_BASE)))
    angles = positions.astype(jnp.float32)[:, None] * frequency[None, :]
    cosine = jnp.cos(angles)[:, None, :]
    sine_of = jnp.sin(angles)[:, None, :]
    front_half = vectors[..., :half_width]
    back_half = vectors[..., half_width:]
    return jnp.concatenate([front_half * cosine - back_half * sine_of, back_half * cosine + front_half * sine_of], axis=-1)


def closure(parents):
    node_count = parents.shape[-1]
    node_ids = jnp.arange(node_count, dtype=jnp.int32)
    reached = (parents[:, :, None] == node_ids[None, None, :]).astype(jnp.float32)
    reached = reached + jnp.eye(node_count, dtype=jnp.float32)[None]
    for level_index in range(max(1, (node_count - 1).bit_length())):
        reached = jnp.minimum(jnp.einsum("sij,sjk->sik", reached, reached, precision=lax.Precision.HIGHEST), 1.0)
    return reached


def block_partial(queries, all_keys, all_values, visible):
    row_count = queries.shape[0]
    kv_heads = all_keys.shape[1] // HD
    group_size = queries.shape[1] // all_keys.shape[1]
    row_tops = []
    row_totals = []
    mixtures = []
    for kv_head in range(kv_heads):
        query_block = queries[:, kv_head * group_size * HD:(kv_head + 1) * group_size * HD].reshape(row_count * group_size, HD)
        key_block = all_keys[:, kv_head * HD:(kv_head + 1) * HD]
        value_block = all_values[:, kv_head * HD:(kv_head + 1) * HD]
        scores = lax.dot_general(query_block, key_block, (((1,), (1,)), ((), ())), preferred_element_type=jnp.float32)
        scores = scores.reshape(row_count, group_size, -1) * (HD ** -0.5)
        scores = jnp.where(visible[:, None, :], scores, MASKED_SCORE)
        row_top = jnp.max(scores, axis=-1)
        weights = jnp.where(visible[:, None, :], jnp.exp(scores - row_top[..., None]), 0.0)
        row_total = jnp.sum(weights, axis=-1)
        mixed_rows = jnp.dot(weights.astype(jnp.bfloat16).reshape(row_count * group_size, -1), value_block, preferred_element_type=jnp.float32)
        mixed_rows = mixed_rows.reshape(row_count, group_size, HD) / jnp.maximum(row_total, 1.0)[..., None]
        row_tops.append(row_top)
        row_totals.append(row_total)
        mixtures.append(mixed_rows.reshape(row_count, group_size * HD).astype(jnp.bfloat16))
    return jnp.concatenate(row_tops, axis=1), jnp.concatenate(row_totals, axis=1), jnp.concatenate(mixtures, axis=1)


def finish(tops, totals, parts):
    piece_count, row_count, head_count = tops.shape
    best = jnp.max(tops, axis=0)
    factor = jnp.exp(tops - best[None]) * totals
    denominator = jnp.sum(factor, axis=0)
    numerator = jnp.sum(parts.astype(jnp.float32).reshape(piece_count, row_count, head_count, HD) * factor[..., None], axis=0)
    return (numerator / denominator[..., None]).reshape(row_count, head_count * HD).astype(jnp.bfloat16)


def attend(queries, blocks):
    tops = []
    totals = []
    parts = []
    for keys, values, visible in blocks:
        top, total, part = block_partial(queries, keys, values, visible)
        tops.append(top)
        totals.append(total)
        parts.append(part)
    return finish(jnp.stack(tops), jnp.stack(totals), jnp.stack(parts))


def reference(states, q_weight, kv_weight, o_weight, store_keys, store_values, prefix_len, cache_len, parents):
    row_count = SEQS * NODES
    kv_width = KVH * HD
    store_rows = CTX // N_TP
    block_rows = row_count // N_TP
    row_ids = jnp.arange(row_count, dtype=jnp.int32)
    seq_of = row_ids // NODES
    store_pos = jnp.arange(CTX, dtype=jnp.int32)
    eye_seq = (jnp.arange(SEQS)[:, None] == jnp.arange(SEQS)[None, :]).astype(jnp.float32)

    def project(inputs, positions):
        new_queries = jnp.dot(inputs, q_weight, preferred_element_type=jnp.float32).reshape(row_count, QH, HD)
        new_queries = rotate(new_queries, positions).reshape(row_count, QH * HD).astype(jnp.bfloat16)
        kv_proj = jnp.dot(inputs, kv_weight, preferred_element_type=jnp.float32)
        new_keys = rotate(kv_proj[:, :kv_width].reshape(row_count, KVH, HD), positions).reshape(row_count, kv_width).astype(jnp.bfloat16)
        new_values = kv_proj[:, kv_width:].astype(jnp.bfloat16)
        return new_queries, new_keys, new_values

    prefill_outs = []
    tail_key_list = []
    tail_value_list = []
    for replica in range(N_REP):
        positions = prefix_len[replica] + row_ids
        new_queries, new_keys, new_values = project(states[0, replica], positions)
        blocks = []
        for block in range(N_TP):
            store_lo = block * store_rows
            new_lo = block * block_rows
            store_mask = jnp.broadcast_to(store_pos[None, store_lo:store_lo + store_rows] < prefix_len[replica], (row_count, store_rows))
            causal = row_ids[None, new_lo:new_lo + block_rows] <= row_ids[:, None]
            visible = jnp.concatenate([store_mask, causal], axis=1)
            keys = jnp.concatenate([store_keys[0, replica, store_lo:store_lo + store_rows], new_keys[new_lo:new_lo + block_rows]], axis=0)
            values = jnp.concatenate([store_values[0, replica, store_lo:store_lo + store_rows], new_values[new_lo:new_lo + block_rows]], axis=0)
            blocks.append((keys, values, visible))
        attended = attend(new_queries, blocks)
        prefill_outs.append(jnp.dot(attended, o_weight, preferred_element_type=jnp.float32).astype(jnp.bfloat16))
        tail_key_list.append(new_keys)
        tail_value_list.append(new_values)

    decode_outs = []
    for replica in range(N_REP):
        source_rep = replica
        reached = closure(parents[replica])
        depths = (jnp.sum(reached, axis=-1).astype(jnp.int32) - 1).reshape(row_count)
        seq_lengths = jnp.broadcast_to(cache_len[replica][:, None], (SEQS, NODES)).reshape(row_count)
        base_pos = jnp.where(seq_of == 0, prefix_len[source_rep] + row_count, seq_lengths)
        positions = base_pos + depths
        new_queries, new_keys, new_values = project(states[1, replica], positions)
        tree_mask = (eye_seq[:, None, :, None] * reached[:, :, None, :]).reshape(row_count, row_count) > 0.5
        source_keys = tail_key_list[source_rep]
        source_values = tail_value_list[source_rep]
        blocks = []
        for block in range(N_TP):
            store_lo = block * store_rows
            new_lo = block * block_rows
            block_pos = store_pos[store_lo:store_lo + store_rows]
            store_mask = ((block_pos[None, :] // CACHE) == seq_of[:, None]) & ((block_pos[None, :] % CACHE) < seq_lengths[:, None])
            tail_mask = jnp.broadcast_to((seq_of == 0)[:, None], (row_count, block_rows))
            visible = jnp.concatenate([store_mask, tree_mask[:, new_lo:new_lo + block_rows], tail_mask], axis=1)
            keys = jnp.concatenate([store_keys[1, replica, store_lo:store_lo + store_rows], new_keys[new_lo:new_lo + block_rows], source_keys[new_lo:new_lo + block_rows]], axis=0)
            values = jnp.concatenate([store_values[1, replica, store_lo:store_lo + store_rows], new_values[new_lo:new_lo + block_rows], source_values[new_lo:new_lo + block_rows]], axis=0)
            blocks.append((keys, values, visible))
        attended = attend(new_queries, blocks)
        decode_outs.append(jnp.dot(attended, o_weight, preferred_element_type=jnp.float32).astype(jnp.bfloat16))
    return jnp.stack([jnp.stack(prefill_outs), jnp.stack(decode_outs)])
```

```python
import jax
import jax.numpy as jnp
from jax import lax
from jax.experimental import pallas as pl
from jax.experimental.pallas import tpu as pltpu
from jax.sharding import PartitionSpec as P

HD = 128
SEQS = 4
NODES = 64
CACHE = 1024

ROPE_BASE = 500000.0
START_TOP = -1e30
HIDDEN = -2e30


def closure(parents):
    node_count = parents.shape[-1]
    node_ids = jnp.arange(node_count, dtype=jnp.int32)
    reached = (parents[:, :, None] == node_ids[None, None, :]).astype(jnp.float32)
    reached = reached + jnp.eye(node_count, dtype=jnp.float32)[None]
    for level_index in range(max(1, (node_count - 1).bit_length())):
        reached = jnp.minimum(
            jnp.einsum("sij,sjk->sik", reached, reached, preferred_element_type=jnp.float32), 1.0
        )
    return reached


def angle_tables(positions):
    half_width = HD // 2
    exponent = jnp.arange(half_width, dtype=jnp.float32) * (-2.0 / HD)
    frequency = jnp.exp(exponent * jnp.log(jnp.float32(ROPE_BASE)))
    angles = positions.astype(jnp.float32)[:, None] * frequency[None, :]
    cosine = jnp.cos(angles)
    sine = jnp.sin(angles)
    return jnp.concatenate([cosine, cosine], axis=1), jnp.concatenate([-sine, sine], axis=1)


def project(total, pieces, piece_ids, weight, tables, out_dtype):
    count = len(pieces)
    rows, depth = pieces[0].shape
    width = weight.shape[1]
    has_total = total is not None
    rotated = tables is not None

    def body(ids, *refs):
        refs = list(refs)
        total_ref = refs.pop(0) if has_total else None
        piece_refs = [refs.pop(0) for _ in range(count)]
        weight_ref = refs.pop(0)
        table_refs = [refs.pop(0) for _ in range(2)] if rotated else None
        out_ref, held, sems = refs
        copies = []
        for p in range(count):
            start = pl.multiple_of(ids[p] * depth, depth)
            copies.append(
                pltpu.make_async_copy(weight_ref.at[pl.ds(start, depth), :], held.at[p], sems.at[p])
            )
            copies[-1].start()
        acc = total_ref[...] if has_total else None
        for p in range(count):
            copies[p].wait()
            term = jnp.dot(piece_refs[p][...], held[p], preferred_element_type=jnp.float32)
            acc = term if acc is None else acc + term
        if rotated:
            cosine = table_refs[0][...]
            sine = table_refs[1][...]
            for h in range(width // HD):
                head = acc[:, h * HD : (h + 1) * HD]
                turned = head * cosine + pltpu.roll(head, HD // 2, 1) * sine
                out_ref[:, h * HD : (h + 1) * HD] = turned.astype(out_dtype)
        else:
            out_ref[...] = acc.astype(out_dtype)

    whole = pl.BlockSpec(memory_space=pltpu.VMEM)
    specs = ([whole] if has_total else []) + [whole] * count
    specs += [pl.BlockSpec(memory_space=pl.ANY)] + ([whole] * 2 if rotated else [])
    args = ([total] if has_total else []) + list(pieces) + [weight] + (list(tables) if rotated else [])
    return pl.pallas_call(
        body,
        out_shape=jax.ShapeDtypeStruct((rows, width), out_dtype),
        grid_spec=pltpu.PrefetchScalarGridSpec(
            num_scalar_prefetch=1,
            grid=(1,),
            in_specs=specs,
            out_specs=whole,
            scratch_shapes=[
                pltpu.VMEM((count, depth, width), weight.dtype),
                pltpu.SemaphoreType.DMA((count,)),
            ],
        ),
        cost_estimate=pl.CostEstimate(
            flops=2 * rows * depth * width * count,
            bytes_accessed=2 * count * depth * (rows + width),
            transcendentals=0,
        ),
    )(piece_ids, *args)


def attend(queries, caches, limits, firsts, lasts, fresh, bias, tails, decoding):
    rows, width = queries.shape
    heads = width // HD
    count = len(caches)
    stored = caches[0].shape[0]
    lines = heads * NODES
    scale = HD ** (-0.5)

    def body(limit_ref, first_ref, last_ref, flag_ref, q_ref, *refs):
        cache_refs = refs[:count]
        fresh_ref, bias_ref, tail_ref, out_ref, top_ref, total_ref, acc_ref = refs[count:]

        def q_of(g):
            start = pl.multiple_of(g * NODES, NODES)
            return jnp.concatenate(
                [q_ref[pl.ds(start, NODES), h * HD : (h + 1) * HD] for h in range(heads)], axis=0
            )

        def update(g, scores, values):
            top = top_ref[g]
            new_top = jnp.maximum(top, jnp.max(scores, axis=1, keepdims=True))
            shrink = jnp.exp(top - new_top)
            weights = jnp.exp(scores - new_top[:, :1])
            total_ref[g] = total_ref[g] * shrink + jnp.sum(weights, axis=1, keepdims=True)
            mixed = jnp.dot(weights.astype(jnp.bfloat16), values, preferred_element_type=jnp.float32)
            acc_ref[g] = acc_ref[g] * shrink + mixed
            top_ref[g] = new_top

        def scores_of(g, keys):
            return lax.dot_general(
                q_of(g), keys, (((1,), (1,)), ((), ())), preferred_element_type=jnp.float32
            ) * scale

        top_ref[...] = jnp.full(top_ref.shape, START_TOP, jnp.float32)
        total_ref[...] = jnp.zeros(total_ref.shape, jnp.float32)
        acc_ref[...] = jnp.zeros(acc_ref.shape, jnp.float32)

        for p in range(count):
            limit = limit_ref[p]

            @pl.when(limit > 0)
            def _(p=p, limit=limit):
                column = lax.broadcasted_iota(jnp.int32, (1, stored), 1)
                hide = jnp.where(column < limit, 0.0, HIDDEN)

                def one(g, carry):
                    update(g, scores_of(g, cache_refs[p][:, :HD]) + hide, cache_refs[p][:, HD:])
                    return carry

                lax.fori_loop(first_ref[p], last_ref[p], one, 0)

        def one_fresh(g, carry):
            hide = bias_ref[pl.ds(pl.multiple_of(g * NODES, NODES), NODES), :]
            hide = jnp.concatenate([hide] * heads, axis=0)
            update(g, scores_of(g, fresh_ref[:, :HD]) + hide, fresh_ref[:, HD:])
            return carry

        lax.fori_loop(0, SEQS, one_fresh, 0)

        @pl.when(flag_ref[0] > 0)
        def _():
            update(0, scores_of(0, tail_ref[:, :HD]), tail_ref[:, HD:])

        def finish(g, carry):
            done = (acc_ref[g] / total_ref[g]).astype(jnp.bfloat16)
            start = pl.multiple_of(g * NODES, NODES)
            for h in range(heads):
                out_ref[pl.ds(start, NODES), h * HD : (h + 1) * HD] = done[h * NODES : (h + 1) * NODES]
            return carry

        lax.fori_loop(0, SEQS, finish, 0)

    whole = pl.BlockSpec(memory_space=pltpu.VMEM)
    return pl.pallas_call(
        body,
        out_shape=jax.ShapeDtypeStruct((rows, width), jnp.bfloat16),
        grid_spec=pltpu.PrefetchScalarGridSpec(
            num_scalar_prefetch=4,
            grid=(1,),
            in_specs=[whole] * (count + 4),
            out_specs=whole,
            scratch_shapes=[pltpu.VMEM((SEQS, lines, HD), jnp.float32)] * 3,
        ),
        cost_estimate=pl.CostEstimate(
            flops=4 * rows * width * stored * count,
            bytes_accessed=4 * count * stored * HD,
            transcendentals=rows * heads * stored * count,
        ),
    )(limits, firsts, lasts, decoding, queries, *caches, fresh, bias, tails)


def bits_of(count):
    return [1 << b for b in reversed(range(count.bit_length() - 1))]


def per_device(
    states, q_weight, kv_weight, o_weight, store_keys, store_values, prefix_len, cache_len, parents
):
    inputs = states[0, 0]
    row_count = inputs.shape[0]
    tp_count = lax.axis_size("tp")
    tp_index = lax.axis_index("tp")
    replica = lax.axis_index("rep")
    section = lax.axis_index("section")
    section_count = lax.axis_size("section")
    decoding = section == 1
    kv_width = kv_weight.shape[1] // 2
    z_count = kv_width // HD
    y_count = tp_count // z_count
    z_index = tp_index // y_count
    store_rows = store_keys.shape[2]

    def swap(block, dz, dy, name):
        route = [
            (z * y_count + y, (z ^ dz) * y_count + (y ^ dy))
            for z in range(z_count)
            for y in range(y_count)
        ]
        with jax.named_scope(name):
            return lax.ppermute(block, "tp", route)

    def along_y(block, dz, name):
        found = [((dz, 0), block)]
        for bit in bits_of(y_count):
            found += [((dz, dy ^ bit), swap(b, 0, bit, f"{name}_y{dz}_{dy ^ bit}")) for (_, dy), b in found]
        return found

    def gathered(block, name):
        along_z = [(0, block)]
        for bit in bits_of(z_count):
            along_z += [(dz ^ bit, swap(b, bit, 0, f"{name}_z{dz ^ bit}")) for dz, b in along_z]
        found = []
        for dz, b in sorted(along_z, key=lambda entry: entry[0]):
            found += along_y(b, dz, name)
        ids = [tp_index ^ (dz * y_count + dy) for (dz, dy), _ in found]
        return [b for _, b in found], jnp.stack(ids).astype(jnp.int32)

    row_ids = jnp.arange(row_count, dtype=jnp.int32)
    seq_of = row_ids // NODES
    own_prefix = prefix_len[replica]
    reached = closure(parents[0])
    depths = (jnp.sum(reached, axis=-1).astype(jnp.int32) - 1).reshape(row_count)
    seq_lengths = jnp.broadcast_to(cache_len[0][:, None], (SEQS, NODES)).reshape(row_count)
    tree_base = jnp.where(seq_of == 0, own_prefix + row_count, seq_lengths)
    positions = jnp.where(decoding, tree_base + depths, own_prefix + row_ids)
    tables = angle_tables(positions)
    eye_seq = (jnp.arange(SEQS)[:, None] == jnp.arange(SEQS)[None, :]).astype(jnp.float32)
    tree_full = (eye_seq[:, None, :, None] * reached[:, :, None, :]).reshape(row_count, row_count)
    seen = jnp.where(decoding, tree_full > 0.5, row_ids[None, :] <= row_ids[:, None])
    bias = jnp.where(seen, 0.0, HIDDEN)

    pieces, piece_ids = gathered(inputs, "x")
    queries = project(None, pieces, piece_ids, q_weight, tables, jnp.bfloat16)

    kv_sums = jnp.dot(inputs, kv_weight, preferred_element_type=jnp.float32).astype(jnp.bfloat16)

    def head_of(keys, values, head):
        start = head * HD
        return jnp.concatenate(
            [
                lax.dynamic_slice_in_dim(keys, start, HD, 1),
                lax.dynamic_slice_in_dim(values, start, HD, 1),
            ],
            axis=1,
        )

    fresh_sum = head_of(kv_sums[:, :kv_width], kv_sums[:, kv_width:], z_index).astype(jnp.float32)
    for dz in range(1, z_count):
        part = head_of(kv_sums[:, :kv_width], kv_sums[:, kv_width:], z_index ^ dz)
        fresh_sum = fresh_sum + swap(part, dz, 0, f"kv_z{dz}").astype(jnp.float32)
    for bit in bits_of(y_count):
        fresh_sum = fresh_sum + swap(fresh_sum.astype(jnp.bfloat16), 0, bit, f"kv_y{bit}").astype(
            jnp.float32
        )
    new_keys = fresh_sum[:, :HD] * tables[0] + jnp.roll(fresh_sum[:, :HD], HD // 2, 1) * tables[1]
    fresh = jnp.concatenate([new_keys, fresh_sum[:, HD:]], axis=1).astype(jnp.bfloat16)
    with jax.named_scope("tail"):
        tails = lax.ppermute(
            fresh, "section", [(s, (s + 1) % section_count) for s in range(section_count)]
        )

    caches = []
    cache_ids = []
    for dz in range(z_count):
        part = head_of(store_keys[0, 0], store_values[0, 0], z_index ^ dz)
        if dz:
            part = swap(part, dz, 0, f"c_z{dz}")
        for (_, dy), b in along_y(part, dz, "c"):
            caches.append(b)
            cache_ids.append(tp_index ^ (dz * y_count + dy))
    base = jnp.stack(cache_ids).astype(jnp.int32) * store_rows
    seqs = base // CACHE
    limits = jnp.where(decoding, cache_len[0][seqs] - base % CACHE, own_prefix - base)
    firsts = jnp.where(decoding, seqs, 0).astype(jnp.int32)
    lasts = jnp.where(decoding, seqs + 1, SEQS).astype(jnp.int32)

    own = attend(
        queries,
        caches,
        limits.astype(jnp.int32),
        firsts,
        lasts,
        fresh,
        bias,
        tails,
        decoding.astype(jnp.int32)[None],
    )
    pieces, piece_ids = gathered(own, "o")
    result = project(None, pieces, piece_ids, o_weight, None, jnp.bfloat16)
    return result[None, None]


def solution(mesh):
    in_specs = (
        P("section", "rep", None, "tp"),
        P(None, "tp"),
        P("tp", None),
        P(None, "tp"),
        P("section", "rep", "tp", None),
        P("section", "rep", "tp", None),
        P(),
        P("rep", None),
        P("rep", None, None),
    )
    out_specs = P("section", "rep", None, "tp")
    return jax.shard_map(
        per_device, mesh=mesh, in_specs=in_specs, out_specs=out_specs, check_vma=False
    )
```
